32 devices in a mesh: pipe: 4 (over y, x), expert: 8 (over z, core).
Axes of the slice: x: 2, y: 2, z: 4, core: 2. Of those that a mesh axis runs over, the one named last changes fastest.
Arguments:
- fwd_in: bfloat16 [4, 1024, 2048], P('pipe', 'expert'), may hold values from -6 to 6
- route_fwd: int32 [4, 1024, 2], P('pipe', 'expert'), may hold values from 0 to 7, as said below
- gate_fwd: float32 [4, 1024, 2], P('pipe', 'expert'), may hold values from 0.1 to 0.9
- bwd_in: bfloat16 [4, 1024, 2048], P('pipe', 'expert'), may hold values from -6 to 6
- bwd_grad: bfloat16 [4, 1024, 2048], P('pipe', 'expert'), may hold values from -6 to 6
- route_bwd: int32 [4, 1024, 2], P('pipe', 'expert'), may hold values from 0 to 7, as said below
- gate_bwd: float32 [4, 1024, 2], P('pipe', 'expert'), may hold values from 0.1 to 0.9
- replica_plan: int32 [4, 4], P('pipe'), may hold values from 0 to 7, as said below
- norm_gain: float32 [4, 2048], P('pipe'), may hold values from 0.25 to 1.75
- expert_weights: bfloat16 [4, 8, 3, 768, 2048], P('pipe', 'expert'), may hold values from -0.125 to 0.125
Outputs:
- next_in: bfloat16 [4, 1024, 2048], P('pipe', 'expert')
- prev_grad: bfloat16 [4, 1024, 2048], P('pipe', 'expert')
The draws below stay inside these ranges and needn't reach their ends.
Inputs may be any that keep to these rules, and one draw needn't show every extreme that they name: `route_fwd`: the 2 experts of a token are different. `route_bwd`: the 2 experts of a token are different. `replica_plan`: in each layer the 3 hosts are different experts, none equal to the first entry.
All inputs are finite; a program needn't handle non-finite values.
Results may differ from the reference program's by a relative error of at most 0.0048.
Values may be sent and summed in bfloat16 or wider, within the bound.
No kernel may reach another device: no remote copies, remote signals or barrier semaphores. Data moves between devices by JAX's collectives and lax.ppermute only.
A program may use at most 128 MiB of HBM per device.

```python
import jax
import jax.numpy as jnp
from jax import lax

D = 2048
FF = 768
TOP = 2
REPL = 3
ROWS = 128
LAYERS = 4
EXPERTS = 8
TOKENS = 1024
SLOTS = 48
N_EXPERT = 8


def popularity(key):
    base_key = jax.random.fold_in(key, 5)
    layer_keys = jax.vmap(lambda layer_id: jax.random.fold_in(base_key, layer_id))(jnp.arange(LAYERS, dtype=jnp.int32))
    orders = jax.vmap(lambda one_key: jax.random.permutation(one_key, EXPERTS))(layer_keys).astype(jnp.int32)
    follower = ((orders[:, :1] + 1) % EXPERTS).astype(jnp.int32)
    last_one = orders[:, -1:]
    swapped = jnp.where(orders == follower, last_one, orders)
    column = jnp.arange(EXPERTS, dtype=jnp.int32)[None, :]
    return jnp.where(column == EXPERTS - 1, follower, swapped).astype(jnp.int32)


def rank_weights():
    ranking = jnp.arange(EXPERTS, dtype=jnp.int32)
    return jnp.where(ranking == 0, 6 * EXPERTS, 2 * EXPERTS - ranking).astype(jnp.int32)


def sample_routes(key, salt):
    orders = popularity(key)
    weights_int = rank_weights()
    salted = jax.random.fold_in(key, salt)
    taken_mask = jnp.zeros((LAYERS, TOKENS, EXPERTS), jnp.int32)
    chosen = []
    for member in range(TOP):
        member_key = jax.random.fold_in(salted, member)
        masked = weights_int[None, None, :] * (1 - taken_mask)
        running = jnp.cumsum(masked, axis=-1, dtype=jnp.int32)
        totals = running[..., -1]
        raw_draws = jax.random.randint(member_key, (LAYERS, TOKENS), 0, 1 << 30, dtype=jnp.int32)
        pick_value = raw_draws % totals
        ranked = jnp.sum((running <= pick_value[..., None]).astype(jnp.int32), axis=-1, dtype=jnp.int32)
        taken_mask = taken_mask + (jnp.arange(EXPERTS, dtype=jnp.int32)[None, None, :] == ranked[..., None]).astype(jnp.int32)
        chosen.append(ranked)
    rank_ids = jnp.stack(chosen, axis=-1)
    widened = jnp.broadcast_to(orders[:, None, :], (LAYERS, TOKENS, EXPERTS))
    return jnp.take_along_axis(widened, rank_ids, axis=-1).astype(jnp.int32)


def draw_route_fwd(key, part):
    return sample_routes(key, 31)


def draw_route_bwd(key, part):
    return sample_routes(key, 37)


def draw_replica_plan(key, part):
    orders = popularity(key)
    return jnp.concatenate([orders[:, :1], orders[:, ::-1][:, :REPL]], axis=1).astype(jnp.int32)


def steps_of(stream_key, extent, cuts, low, largest):
    level, own = 1.0, jax.random.fold_in(stream_key, 6)
    for dim, blocks in cuts:
        steps = jnp.exp(jax.random.uniform(jax.random.fold_in(own, dim), (blocks,), jnp.float32, low / len(cuts), largest / len(cuts)))
        level = level * jnp.repeat(steps, extent[dim] // blocks).reshape([-1 if axis == dim else 1 for axis in range(len(extent))])
    return level


def bell_draw(key, extent, deviation, most, split=(), kind=jnp.bfloat16):
    entries = jax.random.normal(key, extent, jnp.float32) * deviation
    if len(split) > 0:
        entries = steps_of(key, extent, split, -0.22, 0.18) * entries
    return jnp.clip(entries, min=-most, max=most).astype(kind)


def setup_inputs(seed: int = 0) -> dict:
    arg_keys = jax.random.split(jax.random.key(seed), 11)
    return {
        "fwd_in": bell_draw(arg_keys[0], (LAYERS, TOKENS, D), 1.0, 6.0, ((0, 4), (1, 8))),
        "route_fwd": draw_route_fwd(jax.random.fold_in(arg_keys[10], 71), 0),
        "gate_fwd": jnp.clip(0.1 + 0.79999997 * jax.random.uniform(arg_keys[2], (LAYERS, TOKENS, TOP), jnp.float32) ** steps_of(arg_keys[2], (LAYERS, TOKENS, TOP), ((0, 4), (1, 8)), -0.2, 0.2), 0.1, 0.9),
        "bwd_in": bell_draw(arg_keys[3], (LAYERS, TOKENS, D), 1.0, 6.0, ((0, 4), (1, 8))),
        "bwd_grad": bell_draw(arg_keys[4], (LAYERS, TOKENS, D), 1.0, 6.0, ((0, 4), (1, 8))),
        "route_bwd": draw_route_bwd(jax.random.fold_in(arg_keys[10], 71), 0),
        "gate_bwd": jnp.clip(0.1 + 0.79999997 * jax.random.uniform(arg_keys[6], (LAYERS, TOKENS, TOP), jnp.float32) ** steps_of(arg_keys[6], (LAYERS, TOKENS, TOP), ((0, 4), (1, 8)), -0.2, 0.2), 0.1, 0.9),
        "replica_plan": draw_replica_plan(jax.random.fold_in(arg_keys[10], 71), 0),
        "norm_gain": jnp.clip(1.0 + 0.15 * jax.random.normal(arg_keys[8], (LAYERS, D), jnp.float32), 0.25, 1.75),
        "expert_weights": bell_draw(arg_keys[9], (LAYERS, EXPERTS, 3, FF, D), D ** -0.5, 0.125, ((0, 4), (1, 8))),
    }


EPSILON = 1e-06

def normalize(values, norm_scale):
    floats = values.astype(jnp.float32)
    inverse_rms = lax.rsqrt(lax.optimization_barrier(jnp.mean(floats * floats, axis=-1, keepdims=True)) + EPSILON)
    return (floats * inverse_rms * norm_scale).astype(jnp.bfloat16)

def norm_back(values, norm_scale, gradient):
    floats = values.astype(jnp.float32)
    inverse_rms = lax.rsqrt(lax.optimization_barrier(jnp.mean(floats * floats, axis=-1, keepdims=True)) + EPSILON)
    scaled = gradient * norm_scale
    return inverse_rms * scaled - floats * inverse_rms ** 3 * lax.optimization_barrier(jnp.mean(floats * scaled, axis=-1, keepdims=True))

def place_slots(routing, popular, helpers, devices, capacity):
    experts = jnp.arange(devices, dtype=jnp.int32)
    onehot = (routing[:, None] == experts[None, :]).astype(jnp.int32)
    before = (jnp.cumsum(onehot, axis=0, dtype=jnp.int32) - onehot).astype(jnp.int32)
    ranking = lax.optimization_barrier(jnp.sum(before * onehot, axis=1, dtype=jnp.int32))
    per_expert = lax.optimization_barrier(jnp.sum(onehot, axis=0, dtype=jnp.int32))
    host_hit = (helpers[:, None] == experts[None, :]).astype(jnp.int32)
    occupied = jnp.minimum(lax.optimization_barrier(jnp.sum(host_hit * per_expert[None, :], axis=1, dtype=jnp.int32)), capacity)
    spare_rows = (capacity - occupied).astype(jnp.int32)
    spare_ends = jnp.cumsum(spare_rows, dtype=jnp.int32)
    spare_starts = (spare_ends - spare_rows).astype(jnp.int32)
    overflow = (ranking - capacity).astype(jnp.int32)
    host_slot = lax.optimization_barrier(jnp.sum((overflow[:, None] >= spare_ends[None, :]).astype(jnp.int32), axis=1, dtype=jnp.int32))
    home_ok = ranking < capacity
    spill_ok = (routing == popular) & jnp.logical_not(home_ok) & (host_slot < helpers.shape[0])
    chosen = (host_slot[:, None] == jnp.arange(helpers.shape[0], dtype=jnp.int32)[None, :]).astype(jnp.int32)
    spill_device = lax.optimization_barrier(jnp.sum(chosen * helpers[None, :], axis=1, dtype=jnp.int32))
    spill_place = lax.optimization_barrier(jnp.sum(chosen * (occupied - spare_starts)[None, :], axis=1, dtype=jnp.int32)) + overflow
    target = jnp.where(home_ok, routing * capacity + ranking, spill_device * capacity + spill_place)
    target = jnp.where(home_ok | spill_ok, target, -1).astype(jnp.int32)
    anchor = jnp.where(home_ok, 1, 2).astype(jnp.int32)
    return (target, anchor)

def expert_forward(pieces, weights):
    inputs = pieces[0]
    gate_pre = jnp.einsum('bd,fd->bf', inputs, weights[0], preferred_element_type=jnp.float32)
    up_pre = jnp.einsum('bd,fd->bf', inputs, weights[1], preferred_element_type=jnp.float32)
    sigmoid_gate = 1.0 / (1.0 + jnp.exp(-gate_pre))
    hidden = (gate_pre * sigmoid_gate * up_pre).astype(jnp.bfloat16)
    return jnp.dot(hidden, weights[2], preferred_element_type=jnp.float32).astype(jnp.bfloat16)

def expert_backward(pieces, weights):
    inputs, grad_rows = pieces
    gate_pre = jnp.einsum('bd,fd->bf', inputs, weights[0], preferred_element_type=jnp.float32)
    up_pre = jnp.einsum('bd,fd->bf', inputs, weights[1], preferred_element_type=jnp.float32)
    back_hidden = jnp.einsum('bd,fd->bf', grad_rows, weights[2], preferred_element_type=jnp.float32)
    sigmoid_gate = 1.0 / (1.0 + jnp.exp(-gate_pre))
    d_gate = (back_hidden * up_pre * sigmoid_gate * (1.0 + gate_pre * (1.0 - sigmoid_gate))).astype(jnp.bfloat16)
    d_up = (back_hidden * gate_pre * sigmoid_gate).astype(jnp.bfloat16)
    summed = jnp.dot(d_gate, weights[0], preferred_element_type=jnp.float32) + jnp.dot(d_up, weights[1], preferred_element_type=jnp.float32)
    return summed.astype(jnp.bfloat16)

def spread_slots(routing, popular, helpers):
    per_source = routing.reshape(N_EXPERT, ROWS * TOP).astype(jnp.int32)
    targets, anchors = jax.vmap(lambda routes_row: place_slots(routes_row, popular, helpers, N_EXPERT, SLOTS))(per_source)
    bucket = N_EXPERT * SLOTS
    sources = jnp.arange(N_EXPERT, dtype=jnp.int32)[:, None]
    where_to = jnp.where(targets >= 0, targets // SLOTS * bucket + sources * SLOTS + targets % SLOTS, N_EXPERT * bucket).astype(jnp.int32)
    slot_ids = (sources * (ROWS * TOP) + jnp.arange(ROWS * TOP, dtype=jnp.int32)[None, :]).astype(jnp.int32)
    filled = jnp.full((N_EXPERT * bucket,), -1, jnp.int32).at[where_to.reshape(-1)].set(slot_ids.reshape(-1), mode='drop')
    anchor_all = jnp.zeros((N_EXPERT * bucket,), jnp.int32).at[where_to.reshape(-1)].set(anchors.reshape(-1), mode='drop')
    return (where_to, filled.reshape(N_EXPERT, bucket), anchor_all.reshape(N_EXPERT, bucket))

def host_pieces(tables, sources_row):
    present = sources_row >= 0
    clipped = jnp.maximum(sources_row, 0)
    return tuple((jnp.where(present[:, None], table[clipped // stride], jnp.zeros((), table.dtype)) for table, stride in tables))

def run_hosts(function, tables, filled, anchor_all, weights, popular, helpers):

    def one_host(packed):
        host_id, sources_row = packed
        return function(host_pieces(tables, sources_row), weights[host_id])
    outputs = lax.map(one_host, (jnp.arange(N_EXPERT, dtype=jnp.int32), filled))
    for member in range(REPL):
        helper = helpers[member]
        hot_out = function(host_pieces(tables, filled[helper]), weights[popular])
        spilled = anchor_all[helper] == 2
        outputs = outputs.at[helper].set(jnp.where(spilled[:, None], hot_out, outputs[helper]))
    return outputs.reshape(-1, outputs.shape[-1])

def collect(flat_out, where_to):
    limit = flat_out.shape[0]
    picked = flat_out[jnp.minimum(where_to, limit - 1)]
    picked = jnp.where((where_to < limit)[..., None], picked, jnp.zeros((), flat_out.dtype))
    return picked.reshape(TOKENS, TOP, flat_out.shape[-1])

def reference(fwd_in, route_fwd, gate_fwd, bwd_in, bwd_grad, route_bwd, gate_bwd, replica_plan, norm_gain, expert_weights):
    outputs_fwd = []
    outputs_bwd = []
    for layer_id in range(LAYERS):
        weights = expert_weights[layer_id]
        popular = replica_plan[layer_id, 0]
        helpers = replica_plan[layer_id, 1:]
        gain_row = norm_gain[layer_id]
        normed_fwd = normalize(fwd_in[layer_id], gain_row)
        where_fwd, filled_fwd, anchor_fwd = spread_slots(route_fwd[layer_id], popular, helpers)
        flat_fwd = run_hosts(expert_forward, ((normed_fwd, TOP),), filled_fwd, anchor_fwd, weights, popular, helpers)
        expert_out = collect(flat_fwd, where_fwd)
        mixed = lax.optimization_barrier(jnp.sum(gate_fwd[layer_id][:, :, None] * expert_out.astype(jnp.float32), axis=1))
        outputs_fwd.append((fwd_in[layer_id].astype(jnp.float32) + mixed).astype(jnp.bfloat16))
        normed_bwd = normalize(bwd_in[layer_id], gain_row)
        scaled_grad = (gate_bwd[layer_id][:, :, None] * bwd_grad[layer_id].astype(jnp.float32)[:, None, :]).astype(jnp.bfloat16)
        scaled_grad = scaled_grad.reshape(TOKENS * TOP, D)
        where_bwd, filled_bwd, anchor_bwd = spread_slots(route_bwd[layer_id], popular, helpers)
        flat_bwd = run_hosts(expert_backward, ((normed_bwd, TOP), (scaled_grad, 1)), filled_bwd, anchor_bwd, weights, popular, helpers)
        slot_grad = collect(flat_bwd, where_bwd)
        normed_grad = lax.optimization_barrier(jnp.sum(slot_grad.astype(jnp.float32), axis=1))
        input_grad = bwd_grad[layer_id].astype(jnp.float32) + norm_back(bwd_in[layer_id], gain_row, normed_grad)
        outputs_bwd.append(input_grad.astype(jnp.bfloat16))
    next_in = jnp.roll(jnp.stack(outputs_fwd, axis=0), 1, axis=0)
    prev_grad = jnp.roll(jnp.stack(outputs_bwd, axis=0), -1, axis=0)
    return (next_in, prev_grad)
```

```python
import jax
import jax.numpy as jnp
from jax import lax
from jax.experimental import pallas as pl
from jax.experimental.pallas import tpu as pltpu
from jax.sharding import PartitionSpec as P

EPSILON = 1e-06


def broadcast(block, axis, owner):
    block = jnp.where(lax.axis_index(axis) == owner, block, jnp.zeros_like(block))
    return lax.psum(block, axis)


def from_behind(value, axis, steps):
    count = lax.axis_size(axis)
    pairs = [(source, (source + steps) % count) for source in range(count)]
    return lax.ppermute(value, axis, pairs)


def normalize(values, norm_scale):
    floats = values.astype(jnp.float32)
    inverse_rms = lax.rsqrt(jnp.mean(floats * floats, axis=-1, keepdims=True) + EPSILON)
    return (floats * inverse_rms * norm_scale).astype(jnp.bfloat16)


def norm_back(values, norm_scale, gradient):
    floats = values.astype(jnp.float32)
    inverse_rms = lax.rsqrt(jnp.mean(floats * floats, axis=-1, keepdims=True) + EPSILON)
    scaled = gradient * norm_scale
    return inverse_rms * scaled - floats * inverse_rms**3 * jnp.mean(
        floats * scaled, axis=-1, keepdims=True
    )


def place_slots(routing, popular, helpers, devices, capacity):
    experts = jnp.arange(devices, dtype=jnp.int32)
    onehot = (routing[:, None] == experts[None, :]).astype(jnp.int32)
    before = jnp.cumsum(onehot, axis=0, dtype=jnp.int32) - onehot
    ranking = jnp.sum(before * onehot, axis=1, dtype=jnp.int32)
    per_expert = jnp.sum(onehot, axis=0, dtype=jnp.int32)
    host_hit = (helpers[:, None] == experts[None, :]).astype(jnp.int32)
    occupied = jnp.minimum(
        jnp.sum(host_hit * per_expert[None, :], axis=1, dtype=jnp.int32), capacity
    )
    spare_rows = capacity - occupied
    spare_ends = jnp.cumsum(spare_rows, dtype=jnp.int32)
    spare_starts = spare_ends - spare_rows
    overflow = ranking - capacity
    host_slot = jnp.sum(
        (overflow[:, None] >= spare_ends[None, :]).astype(jnp.int32), axis=1, dtype=jnp.int32
    )
    home_ok = ranking < capacity
    spill_ok = (routing == popular) & jnp.logical_not(home_ok) & (host_slot < helpers.shape[0])
    chosen = (host_slot[:, None] == jnp.arange(helpers.shape[0], dtype=jnp.int32)[None, :]).astype(
        jnp.int32
    )
    spill_device = jnp.sum(chosen * helpers[None, :], axis=1, dtype=jnp.int32)
    spill_place = (
        jnp.sum(chosen * (occupied - spare_starts)[None, :], axis=1, dtype=jnp.int32) + overflow
    )
    target = jnp.where(home_ok, routing * capacity + ranking, spill_device * capacity + spill_place)
    target = jnp.where(home_ok | spill_ok, target, -1)
    anchor = jnp.where(home_ok, 1, 2).astype(jnp.int32)
    return (target, anchor)


def expert_forward(pieces, weights):
    inputs = pieces[0]
    gate_pre = jnp.einsum("bd,fd->bf", inputs, weights[0], preferred_element_type=jnp.float32)
    up_pre = jnp.einsum("bd,fd->bf", inputs, weights[1], preferred_element_type=jnp.float32)
    sigmoid_gate = 1.0 / (1.0 + jnp.exp(-gate_pre))
    hidden = (gate_pre * sigmoid_gate * up_pre).astype(jnp.bfloat16)
    return jnp.dot(hidden, weights[2], preferred_element_type=jnp.float32).astype(jnp.bfloat16)


def expert_backward(pieces, weights):
    inputs, grad_rows = pieces
    gate_pre = jnp.einsum("bd,fd->bf", inputs, weights[0], preferred_element_type=jnp.float32)
    up_pre = jnp.einsum("bd,fd->bf", inputs, weights[1], preferred_element_type=jnp.float32)
    back_hidden = jnp.einsum("bd,fd->bf", grad_rows, weights[2], preferred_element_type=jnp.float32)
    sigmoid_gate = 1.0 / (1.0 + jnp.exp(-gate_pre))
    d_gate = (back_hidden * up_pre * sigmoid_gate * (1.0 + gate_pre * (1.0 - sigmoid_gate))).astype(
        jnp.bfloat16
    )
    d_up = (back_hidden * gate_pre * sigmoid_gate).astype(jnp.bfloat16)
    summed = jnp.dot(d_gate, weights[0], preferred_element_type=jnp.float32) + jnp.dot(
        d_up, weights[1], preferred_element_type=jnp.float32
    )
    return summed.astype(jnp.bfloat16)


def build_rows(tables, target, devices, capacity):
    count = target.shape[0]
    total = devices * capacity
    safe_target = jnp.where(target >= 0, target, total)
    source_of = (
        jnp.full((total,), -1, jnp.int32)
        .at[safe_target]
        .set(jnp.arange(count, dtype=jnp.int32), mode="drop")
    )
    present = source_of >= 0
    clipped = jnp.maximum(source_of, 0)
    built = []
    for table, stride in tables:
        rows_here = jnp.where(
            present[:, None], table[clipped // stride], jnp.zeros((), table.dtype)
        )
        built.append(rows_here.reshape(devices, capacity, table.shape[-1]))
    return (tuple(built), safe_target)


def build_tags(anchor, safe_target, devices, capacity):
    tags = jnp.zeros((devices * capacity,), jnp.int32).at[safe_target].set(anchor, mode="drop")
    return tags.astype(jnp.bfloat16).reshape(devices, capacity)


def grouped(function, inputs, tags, own_weights, hot_weights):
    total = tags.shape[0]
    features = inputs[0].shape[-1]
    anchor = tags.astype(jnp.int32)
    is_own = anchor == 1
    is_hot = anchor == 2
    is_empty = jnp.logical_not(is_own | is_hot)
    own_count = jnp.sum(is_own.astype(jnp.int32), dtype=jnp.int32)
    hot_count = jnp.sum(is_hot.astype(jnp.int32), dtype=jnp.int32)
    own_rank = jnp.cumsum(is_own.astype(jnp.int32), dtype=jnp.int32) - 1
    hot_rank = own_count + jnp.cumsum(is_hot.astype(jnp.int32), dtype=jnp.int32) - 1
    empty_rank = own_count + hot_count + jnp.cumsum(is_empty.astype(jnp.int32), dtype=jnp.int32) - 1
    position = jnp.where(is_own, own_rank, jnp.where(is_hot, hot_rank, empty_rank))
    ordering = jnp.zeros((total,), jnp.int32).at[position].set(jnp.arange(total, dtype=jnp.int32))
    block = 128
    number = total // block
    stacked = tuple(
        (member[ordering].reshape(number, block, member.shape[-1]) for member in inputs)
    )
    empty_out = jnp.zeros((block, features), jnp.bfloat16)

    def one_block(packed):
        pieces, start = packed
        own_out = lax.cond(
            start < own_count, lambda: function(pieces, own_weights), lambda: empty_out
        )
        needs_hot = (start + block > own_count) & (start < own_count + hot_count)
        hot_out = lax.cond(needs_hot, lambda: function(pieces, hot_weights), lambda: empty_out)
        row_ids = start + jnp.arange(block, dtype=jnp.int32)
        return jnp.where((row_ids < own_count)[:, None], own_out, hot_out)

    starts = jnp.arange(number, dtype=jnp.int32) * block
    outputs = lax.map(one_block, (stacked, starts))
    return outputs.reshape(total, features)[position]


def collect(returned, target, tokens_here, top_count):
    flat_back = returned.reshape(-1, returned.shape[-1])
    limit = flat_back.shape[0]
    picked = flat_back[jnp.clip(target, 0, limit - 1)]
    picked = jnp.where((target >= 0)[:, None], picked, jnp.zeros((), flat_back.dtype))
    return picked.reshape(tokens_here, top_count, flat_back.shape[-1])


CHIPS = 4


def along_line(value, chip_pairs):
    pairs = [(2 * a + core, 2 * b + core) for a, b in chip_pairs for core in range(2)]
    return lax.ppermute(value, "expert", pairs)


NEAR = ((0, 1), (1, 0), (2, 3), (3, 2))
MIDDLE = ((1, 2), (2, 1))
OUTWARD = ((1, 0), (2, 3))
INWARD = ((0, 1), (3, 2))
TWO_AWAY = ((0, 2), (2, 0), (1, 3), (3, 1))
MIRROR = ((0, 3), (3, 0), (1, 2), (2, 1))


def accepted_gates(routing, gates, popular, helpers, devices, capacity):
    tokens_here = routing.shape[0]
    experts = jnp.arange(devices, dtype=jnp.int32)
    hits = routing[:, :, None] == experts[None, None, :]
    named = jnp.sum(hits.astype(jnp.float32), axis=1)
    earlier = (
        jnp.arange(tokens_here)[:, None] > jnp.arange(tokens_here)[None, :]
    ).astype(jnp.float32)
    rank = jnp.dot(earlier, named, preferred_element_type=jnp.float32)
    load = jnp.sum(named, axis=0)
    is_host = jnp.sum((helpers[:, None] == experts[None, :]).astype(jnp.float32), axis=0)
    free = jnp.sum(is_host * (capacity - jnp.minimum(load, capacity)))
    limit = capacity + jnp.where(experts == popular, free, 0.0)
    weight = jnp.sum(jnp.where(hits, gates[:, :, None], 0.0), axis=1)
    return jnp.where(rank < limit[None, :], weight, 0.0)


def norm_kernel(values, gain, out):
    floats = values[...].astype(jnp.float32)
    inverse_rms = lax.rsqrt(jnp.mean(floats * floats, axis=-1, keepdims=True) + EPSILON)
    out[...] = (floats * inverse_rms * gain[...]).astype(out.dtype)


def norm_call(values, gain_row):
    return pl.pallas_call(
        norm_kernel,
        out_shape=jax.ShapeDtypeStruct(values.shape, jnp.bfloat16),
        cost_estimate=pl.CostEstimate(
            flops=4 * values.size, bytes_accessed=4 * values.size, transcendentals=0
        ),
        name="norm_rows",
    )(values, gain_row[None])


def column_of(table, column):
    lanes = lax.broadcasted_iota(jnp.int32, table.shape, 1)
    return jnp.sum(jnp.where(lanes == column, table, 0.0), axis=1, keepdims=True)


def across(left, right):
    return lax.dot_general(
        left, right, (((1,), (1,)), ((), ())), preferred_element_type=jnp.float32
    )


def run_experts(info, step, tiles, own, mate, one_tile, finish):
    for member, weights in enumerate((own, mate)):

        @pl.when((step >= member * tiles) & (step < (member + 1) * tiles))
        def _():
            one_tile(weights, info[member], step == member * tiles)

    for member in range(2):

        @pl.when(step == member * tiles + tiles - 1)
        def _():
            finish(info[member], member == 0)


def load_parts(info, parts, places):
    offset = 0
    for part in parts:
        count = part[0][0].shape[0]
        window = pl.ds(offset, count)
        for pair, place in zip(part, places):
            if len(pair) == 1:
                place[window, :] = pair[0][...]
            else:
                place[window, :] = jnp.where(info[2] > 0, pair[1][...], pair[0][...])
        offset += count


def store_parts(value, outs):
    offset = 0
    for out in outs:
        count = out.shape[0]
        out[...] = value[offset : offset + count].astype(out.dtype)
        offset += count


def forward_kernel(tiles, info, parts, own, mate, outs, rows, table, acc, total):
    step = pl.program_id(0)

    @pl.when(step == 0)
    def _():
        load_parts(info, parts, (rows, table))

    def one_tile(weights, expert, first):
        gate_pre = across(rows[...], weights[0])
        up_pre = across(rows[...], weights[1])
        hidden = (gate_pre * (1.0 / (1.0 + jnp.exp(-gate_pre))) * up_pre).astype(jnp.bfloat16)
        part = jnp.dot(hidden, weights[2], preferred_element_type=jnp.float32)
        acc[...] = jnp.where(first, part, acc[...] + part)

    def finish(expert, first):
        gate = column_of(table[...], expert)
        part = gate * acc[...].astype(jnp.bfloat16).astype(jnp.float32)
        if first:
            total[...] = part
        else:
            store_parts(total[...] + part, outs)

    run_experts(info, step, tiles, own, mate, one_tile, finish)


def backward_kernel(tiles, info, parts, own, mate, outs, rows, grad, table, scaled, acc, total):
    step = pl.program_id(0)
    half = table.shape[1] // 2

    @pl.when(step == 0)
    def _():
        load_parts(info, parts, (rows, grad, table))

    def one_tile(weights, expert, first):
        @pl.when(first)
        def _():
            gate = column_of(table[...], half + expert)
            scaled[...] = (gate * grad[...].astype(jnp.float32)).astype(jnp.bfloat16)

        gate_pre = across(rows[...], weights[0])
        up_pre = across(rows[...], weights[1])
        back_hidden = across(scaled[...], weights[2])
        sig = 1.0 / (1.0 + jnp.exp(-gate_pre))
        d_gate = (back_hidden * up_pre * sig * (1.0 + gate_pre * (1.0 - sig))).astype(jnp.bfloat16)
        d_up = (back_hidden * gate_pre * sig).astype(jnp.bfloat16)
        part = jnp.dot(d_gate, weights[0], preferred_element_type=jnp.float32) + jnp.dot(
            d_up, weights[1], preferred_element_type=jnp.float32
        )
        acc[...] = jnp.where(first, part, acc[...] + part)

    def finish(expert, first):
        part = acc[...].astype(jnp.bfloat16).astype(jnp.float32)
        if first:
            total[...] = part
        else:
            store_parts(total[...] + part, outs)

    run_experts(info, step, tiles, own, mate, one_tile, finish)


def expert_call(info, parts, own, mate, out_dtypes):
    backward = len(parts[0]) == 3
    features = parts[0][0][0].shape[1]
    counts = [part[0][0].shape[0] for part in parts]
    total = sum(counts)
    hidden = own.shape[1]
    width = 256 if hidden % 256 == 0 else hidden
    tiles = hidden // width
    flat = [member for part in parts for pair in part for member in pair]

    def whole(value):
        return pl.BlockSpec(value.shape, lambda s, i: (0, 0))

    own_spec = pl.BlockSpec((3, width, features), lambda s, i: (0, jnp.minimum(s, tiles - 1), 0))
    mate_spec = pl.BlockSpec((3, width, features), lambda s, i: (0, jnp.maximum(s - tiles, 0), 0))
    rows = pltpu.VMEM((total, features), jnp.bfloat16)
    wide = pltpu.VMEM((total, features), jnp.float32)
    table = pltpu.VMEM((total, parts[0][-1][0].shape[1]), jnp.float32)
    if backward:
        kernel, scratch, matmuls = backward_kernel, [rows, rows, table, rows, wide, wide], 5
    else:
        kernel, scratch, matmuls = forward_kernel, [rows, table, wide, wide], 3

    def body(info_ref, *refs):
        ins, rest = list(refs[: len(flat)]), refs[len(flat) :]
        nested = [[[ins.pop(0) for _ in pair] for pair in part] for part in parts]
        outs = rest[2 : 2 + len(parts)]
        kernel(tiles, info_ref, nested, rest[0], rest[1], outs, *rest[2 + len(parts) :])

    shapes = [
        jax.ShapeDtypeStruct((count, features), kind) for count, kind in zip(counts, out_dtypes)
    ]
    return pl.pallas_call(
        body,
        out_shape=shapes,
        grid_spec=pltpu.PrefetchScalarGridSpec(
            num_scalar_prefetch=1,
            grid=(2 * tiles,),
            in_specs=[whole(value) for value in flat] + [own_spec, mate_spec],
            out_specs=[whole(shape) for shape in shapes],
            scratch_shapes=scratch,
        ),
        cost_estimate=pl.CostEstimate(
            flops=2 * matmuls * 2 * total * hidden * features,
            bytes_accessed=2 * 2 * own.size,
            transcendentals=2 * total * hidden,
        ),
        compiler_params=pltpu.CompilerParams(vmem_limit_bytes=44 * 1024 * 1024),
        name="backward_experts" if backward else "forward_experts",
    )(info, *flat, own, mate)


def gather_line(value):
    near = along_line(value, NEAR)
    middle = along_line(value, MIDDLE)
    inner = along_line(near, MIDDLE)
    outer_one = along_line(middle, OUTWARD)
    outer_two = along_line(inner, OUTWARD)
    return near, (middle, outer_one), (inner, outer_two)


def add_rows(left, right):
    return (left.astype(jnp.float32) + right.astype(jnp.float32)).astype(jnp.bfloat16)


def scatter_line(own, near, second, third):
    third = add_rows(third, along_line(third, INWARD))
    inner = along_line(third, MIDDLE)
    second = add_rows(second, along_line(second, INWARD))
    middle = along_line(second, MIDDLE)
    near = along_line(add_rows(near, inner), NEAR)
    return own + middle.astype(jnp.float32) + near.astype(jnp.float32)


def gather_shards(
    fwd_in,
    route_fwd,
    gate_fwd,
    bwd_in,
    bwd_grad,
    route_bwd,
    gate_bwd,
    replica_plan,
    norm_gain,
    expert_weights,
):
    devices = lax.axis_size("expert")
    position = lax.axis_index("expert")
    tokens_here = fwd_in.shape[1]
    top_count = route_fwd.shape[2]
    capacity = 3 * tokens_here * top_count // (2 * devices)
    popular = replica_plan[0, 0]
    helpers = replica_plan[0, 1:]
    resident = expert_weights[0, 0]
    gain_row = norm_gain[0]
    mate = lax.ppermute(resident, "expert", [(i, i ^ 1) for i in range(devices)])
    table = jnp.concatenate(
        [
            accepted_gates(route_fwd[0], gate_fwd[0], popular, helpers, devices, capacity),
            accepted_gates(route_bwd[0], gate_bwd[0], popular, helpers, devices, capacity),
        ],
        axis=1,
    )
    table_near = along_line(table, NEAR)
    table_two = along_line(table, TWO_AWAY)
    table_mirror = along_line(table, MIRROR)
    at_end = ((position < 2) | (position >= devices - 2)).astype(jnp.int32)
    info = (
        position * jnp.array([1, 1, 0], jnp.int32)
        + (1 - 2 * (position % 2)) * jnp.array([0, 1, 0], jnp.int32)
        + at_end * jnp.array([0, 0, 1], jnp.int32)
    )
    second_table, third_table = (table_mirror, table_two), (table_two, table_mirror)

    grads = bwd_grad[0]
    normed_bwd = norm_call(bwd_in[0], gain_row)
    normed_fwd = norm_call(fwd_in[0], gain_row)
    wide, narrow = jnp.float32, jnp.bfloat16

    near_g, second_g, third_g = gather_line(grads)
    near_n, second_n, third_n = gather_line(normed_bwd)
    own_b, near_b = expert_call(
        info,
        (((normed_bwd,), (grads,), (table,)), ((near_n,), (near_g,), (table_near,))),
        resident,
        mate,
        (wide, narrow),
    )
    (second_b,) = expert_call(
        info, ((second_n, second_g, second_table),), resident, mate, (narrow,)
    )
    (third_b,) = expert_call(info, ((third_n, third_g, third_table),), resident, mate, (narrow,))
    normed_grad = scatter_line(own_b, near_b, second_b, third_b)
    input_grad = (
        grads.astype(jnp.float32) + norm_back(bwd_in[0], gain_row, normed_grad)
    ).astype(jnp.bfloat16)
    prev_grad = from_behind(input_grad, "pipe", -1)

    near_f = along_line(normed_fwd, NEAR)
    two_f = along_line(normed_fwd, TWO_AWAY)
    mirror_f = along_line(normed_fwd, MIRROR)
    own_f, back_f = expert_call(
        info,
        (((normed_fwd,), (table,)), ((near_f,), (table_near,))),
        resident,
        mate,
        (wide, narrow),
    )
    second_f, third_f = expert_call(
        info,
        (((mirror_f, two_f), second_table), ((two_f, mirror_f), third_table)),
        resident,
        mate,
        (narrow, narrow),
    )
    mixed = scatter_line(own_f, back_f, second_f, third_f)
    layer_out = (fwd_in[0].astype(jnp.float32) + mixed).astype(jnp.bfloat16)
    next_in = from_behind(layer_out, "pipe", 1)
    return (next_in[None], prev_grad[None])


def exchange_shards(
    fwd_in,
    route_fwd,
    gate_fwd,
    bwd_in,
    bwd_grad,
    route_bwd,
    gate_bwd,
    replica_plan,
    norm_gain,
    expert_weights,
):
    devices = lax.axis_size("expert")
    tokens_here = fwd_in.shape[1]
    features = fwd_in.shape[2]
    top_count = route_fwd.shape[2]
    capacity = 3 * tokens_here * top_count // (2 * devices)
    popular = replica_plan[0, 0]
    helpers = replica_plan[0, 1:]
    resident = expert_weights[0, 0]
    own_weights = (resident[0], resident[1], resident[2])
    gain_row = norm_gain[0]
    normed_fwd = normalize(fwd_in[0], gain_row)
    normed_bwd = normalize(bwd_in[0], gain_row)
    scaled_grad = (gate_bwd[0][:, :, None] * bwd_grad[0].astype(jnp.float32)[:, None, :]).astype(
        jnp.bfloat16
    )
    scaled_grad = scaled_grad.reshape(tokens_here * top_count, features)
    target_fwd, anchor_fwd = place_slots(
        route_fwd[0].reshape(-1), popular, helpers, devices, capacity
    )
    target_bwd, anchor_bwd = place_slots(
        route_bwd[0].reshape(-1), popular, helpers, devices, capacity
    )
    built_fwd, safe_fwd = build_rows(((normed_fwd, top_count),), target_fwd, devices, capacity)
    built_bwd, safe_bwd = build_rows(
        ((normed_bwd, top_count), (scaled_grad, 1)), target_bwd, devices, capacity
    )
    tags_fwd = build_tags(anchor_fwd, safe_fwd, devices, capacity)
    tags_bwd = build_tags(anchor_bwd, safe_bwd, devices, capacity)
    recv_fwd, recv_tags_fwd = (
        lax.all_to_all(built_fwd[0], "expert", split_axis=0, concat_axis=0, tiled=True),
        lax.all_to_all(tags_fwd, "expert", split_axis=0, concat_axis=0, tiled=True),
    )
    recv_bwd, recv_grad, recv_tags_bwd = (
        lax.all_to_all(built_bwd[0], "expert", split_axis=0, concat_axis=0, tiled=True),
        lax.all_to_all(built_bwd[1], "expert", split_axis=0, concat_axis=0, tiled=True),
        lax.all_to_all(tags_bwd, "expert", split_axis=0, concat_axis=0, tiled=True),
    )
    fetched = broadcast(resident, "expert", popular)
    hot_weights = (fetched[0], fetched[1], fetched[2])
    slot_total = devices * capacity
    out_fwd = grouped(
        expert_forward,
        (recv_fwd.reshape(slot_total, features),),
        recv_tags_fwd.reshape(slot_total),
        own_weights,
        hot_weights,
    )
    back_fwd = lax.all_to_all(
        out_fwd.reshape(devices, capacity, features),
        "expert",
        split_axis=0,
        concat_axis=0,
        tiled=True,
    )
    expert_out = collect(back_fwd, target_fwd, tokens_here, top_count)
    mixed = jnp.sum(gate_fwd[0][:, :, None] * expert_out.astype(jnp.float32), axis=1)
    layer_out = (fwd_in[0].astype(jnp.float32) + mixed).astype(jnp.bfloat16)
    next_in = from_behind(layer_out, "pipe", 1)
    out_bwd = grouped(
        expert_backward,
        (recv_bwd.reshape(slot_total, features), recv_grad.reshape(slot_total, features)),
        recv_tags_bwd.reshape(slot_total),
        own_weights,
        hot_weights,
    )
    back_bwd = lax.all_to_all(
        out_bwd.reshape(devices, capacity, features),
        "expert",
        split_axis=0,
        concat_axis=0,
        tiled=True,
    )
    slot_grad = collect(back_bwd, target_bwd, tokens_here, top_count)
    normed_grad = jnp.sum(slot_grad.astype(jnp.float32), axis=1)
    input_grad = (
        bwd_grad[0].astype(jnp.float32) + norm_back(bwd_in[0], gain_row, normed_grad)
    ).astype(jnp.bfloat16)
    prev_grad = from_behind(input_grad, "pipe", -1)
    return (next_in[None], prev_grad[None])


def solution(mesh):
    in_specs = (
        P("pipe", "expert", None),
        P("pipe", "expert", None),
        P("pipe", "expert", None),
        P("pipe", "expert", None),
        P("pipe", "expert", None),
        P("pipe", "expert", None),
        P("pipe", "expert", None),
        P("pipe", None),
        P("pipe", None),
        P("pipe", "expert", None, None, None),
    )
    out_specs = (P("pipe", "expert", None), P("pipe", "expert", None))
    gathers = mesh.shape["expert"] == 2 * CHIPS
    plan = gather_shards if gathers else exchange_shards

    return jax.shard_map(plan, mesh=mesh, in_specs=in_specs, out_specs=out_specs, check_vma=False)
```

```python
import jax
import jax.numpy as jnp
from jax import lax
from jax.experimental import pallas as pl
from jax.experimental.pallas import tpu as pltpu
from jax.sharding import PartitionSpec as P

EPSILON = 1e-06


def broadcast(block, axis, owner):
    block = jnp.where(lax.axis_index(axis) == owner, block, jnp.zeros_like(block))
    return lax.psum(block, axis)


def from_behind(value, axis, steps):
    count = lax.axis_size(axis)
    pairs = [(source, (source + steps) % count) for source in range(count)]
    return lax.ppermute(value, axis, pairs)


def normalize(values, norm_scale):
    floats = values.astype(jnp.float32)
    inverse_rms = lax.rsqrt(jnp.mean(floats * floats, axis=-1, keepdims=True) + EPSILON)
    return (floats * inverse_rms * norm_scale).astype(jnp.bfloat16)


def norm_back(values, norm_scale, gradient):
    floats = values.astype(jnp.float32)
    inverse_rms = lax.rsqrt(jnp.mean(floats * floats, axis=-1, keepdims=True) + EPSILON)
    scaled = gradient * norm_scale
    return inverse_rms * scaled - floats * inverse_rms**3 * jnp.mean(
        floats * scaled, axis=-1, keepdims=True
    )


def place_slots(routing, popular, helpers, devices, capacity):
    experts = jnp.arange(devices, dtype=jnp.int32)
    onehot = (routing[:, None] == experts[None, :]).astype(jnp.int32)
    before = jnp.cumsum(onehot, axis=0, dtype=jnp.int32) - onehot
    ranking = jnp.sum(before * onehot, axis=1, dtype=jnp.int32)
    per_expert = jnp.sum(onehot, axis=0, dtype=jnp.int32)
    host_hit = (helpers[:, None] == experts[None, :]).astype(jnp.int32)
    occupied = jnp.minimum(
        jnp.sum(host_hit * per_expert[None, :], axis=1, dtype=jnp.int32), capacity
    )
    spare_rows = capacity - occupied
    spare_ends = jnp.cumsum(spare_rows, dtype=jnp.int32)
    spare_starts = spare_ends - spare_rows
    overflow = ranking - capacity
    host_slot = jnp.sum(
        (overflow[:, None] >= spare_ends[None, :]).astype(jnp.int32), axis=1, dtype=jnp.int32
    )
    home_ok = ranking < capacity
    spill_ok = (routing == popular) & jnp.logical_not(home_ok) & (host_slot < helpers.shape[0])
    chosen = (host_slot[:, None] == jnp.arange(helpers.shape[0], dtype=jnp.int32)[None, :]).astype(
        jnp.int32
    )
    spill_device = jnp.sum(chosen * helpers[None, :], axis=1, dtype=jnp.int32)
    spill_place = (
        jnp.sum(chosen * (occupied - spare_starts)[None, :], axis=1, dtype=jnp.int32) + overflow
    )
    target = jnp.where(home_ok, routing * capacity + ranking, spill_device * capacity + spill_place)
    target = jnp.where(home_ok | spill_ok, target, -1)
    anchor = jnp.where(home_ok, 1, 2).astype(jnp.int32)
    return (target, anchor)


def expert_forward(pieces, weights):
    inputs = pieces[0]
    gate_pre = jnp.einsum("bd,fd->bf", inputs, weights[0], preferred_element_type=jnp.float32)
    up_pre = jnp.einsum("bd,fd->bf", inputs, weights[1], preferred_element_type=jnp.float32)
    sigmoid_gate = 1.0 / (1.0 + jnp.exp(-gate_pre))
    hidden = (gate_pre * sigmoid_gate * up_pre).astype(jnp.bfloat16)
    return jnp.dot(hidden, weights[2], preferred_element_type=jnp.float32).astype(jnp.bfloat16)


def expert_backward(pieces, weights):
    inputs, grad_rows = pieces
    gate_pre = jnp.einsum("bd,fd->bf", inputs, weights[0], preferred_element_type=jnp.float32)
    up_pre = jnp.einsum("bd,fd->bf", inputs, weights[1], preferred_element_type=jnp.float32)
    back_hidden = jnp.einsum("bd,fd->bf", grad_rows, weights[2], preferred_element_type=jnp.float32)
    sigmoid_gate = 1.0 / (1.0 + jnp.exp(-gate_pre))
    d_gate = (back_hidden * up_pre * sigmoid_gate * (1.0 + gate_pre * (1.0 - sigmoid_gate))).astype(
        jnp.bfloat16
    )
    d_up = (back_hidden * gate_pre * sigmoid_gate).astype(jnp.bfloat16)
    summed = jnp.dot(d_gate, weights[0], preferred_element_type=jnp.float32) + jnp.dot(
        d_up, weights[1], preferred_element_type=jnp.float32
    )
    return summed.astype(jnp.bfloat16)


def build_rows(tables, target, devices, capacity):
    count = target.shape[0]
    total = devices * capacity
    safe_target = jnp.where(target >= 0, target, total)
    source_of = (
        jnp.full((total,), -1, jnp.int32)
        .at[safe_target]
        .set(jnp.arange(count, dtype=jnp.int32), mode="drop")
    )
    present = source_of >= 0
    clipped = jnp.maximum(source_of, 0)
    built = []
    for table, stride in tables:
        rows_here = jnp.where(
            present[:, None], table[clipped // stride], jnp.zeros((), table.dtype)
        )
        built.append(rows_here.reshape(devices, capacity, table.shape[-1]))
    return (tuple(built), safe_target)


def build_tags(anchor, safe_target, devices, capacity):
    tags = jnp.zeros((devices * capacity,), jnp.int32).at[safe_target].set(anchor, mode="drop")
    return tags.astype(jnp.bfloat16).reshape(devices, capacity)


def grouped(function, inputs, tags, own_weights, hot_weights):
    total = tags.shape[0]
    features = inputs[0].shape[-1]
    anchor = tags.astype(jnp.int32)
    is_own = anchor == 1
    is_hot = anchor == 2
    is_empty = jnp.logical_not(is_own | is_hot)
    own_count = jnp.sum(is_own.astype(jnp.int32), dtype=jnp.int32)
    hot_count = jnp.sum(is_hot.astype(jnp.int32), dtype=jnp.int32)
    own_rank = jnp.cumsum(is_own.astype(jnp.int32), dtype=jnp.int32) - 1
    hot_rank = own_count + jnp.cumsum(is_hot.astype(jnp.int32), dtype=jnp.int32) - 1
    empty_rank = own_count + hot_count + jnp.cumsum(is_empty.astype(jnp.int32), dtype=jnp.int32) - 1
    position = jnp.where(is_own, own_rank, jnp.where(is_hot, hot_rank, empty_rank))
    ordering = jnp.zeros((total,), jnp.int32).at[position].set(jnp.arange(total, dtype=jnp.int32))
    block = 128
    number = total // block
    stacked = tuple(
        (member[ordering].reshape(number, block, member.shape[-1]) for member in inputs)
    )
    empty_out = jnp.zeros((block, features), jnp.bfloat16)

    def one_block(packed):
        pieces, start = packed
        own_out = lax.cond(
            start < own_count, lambda: function(pieces, own_weights), lambda: empty_out
        )
        needs_hot = (start + block > own_count) & (start < own_count + hot_count)
        hot_out = lax.cond(needs_hot, lambda: function(pieces, hot_weights), lambda: empty_out)
        row_ids = start + jnp.arange(block, dtype=jnp.int32)
        return jnp.where((row_ids < own_count)[:, None], own_out, hot_out)

    starts = jnp.arange(number, dtype=jnp.int32) * block
    outputs = lax.map(one_block, (stacked, starts))
    return outputs.reshape(total, features)[position]


def collect(returned, target, tokens_here, top_count):
    flat_back = returned.reshape(-1, returned.shape[-1])
    limit = flat_back.shape[0]
    picked = flat_back[jnp.clip(target, 0, limit - 1)]
    picked = jnp.where((target >= 0)[:, None], picked, jnp.zeros((), flat_back.dtype))
    return picked.reshape(tokens_here, top_count, flat_back.shape[-1])


CHIPS = 4


def along_line(value, chip_pairs):
    pairs = [(2 * a + core, 2 * b + core) for a, b in chip_pairs for core in range(2)]
    return lax.ppermute(value, "expert", pairs)


def to_section(value, chip_pairs, ahead):
    sections, devices = lax.axis_size("pipe"), lax.axis_size("expert")
    pairs = [
        (section * devices + 2 * a + core, (section + ahead) % sections * devices + 2 * b + core)
        for section in range(sections)
        for a, b in chip_pairs
        for core in range(2)
    ]
    return lax.ppermute(value, ("pipe", "expert"), pairs)


NEAR = ((0, 1), (1, 0), (2, 3), (3, 2))
MIDDLE = ((1, 2), (2, 1))
OUTWARD = ((1, 0), (2, 3))
INWARD = ((0, 1), (3, 2))
HERE = ((0, 0), (1, 1), (2, 2), (3, 3))
SKIP = ((0, 2), (3, 1))
TWO_AWAY = ((0, 2), (2, 0), (1, 3), (3, 1))
MIRROR = ((0, 3), (3, 0), (1, 2), (2, 1))


def accepted_gates(routing, gates, popular, helpers, devices, capacity):
    tokens_here = routing.shape[0]
    experts = jnp.arange(devices, dtype=jnp.int32)
    hits = routing.T[:, None, :] == experts[None, :, None]
    named = jnp.sum(hits.astype(jnp.float32), axis=0)
    later = (
        jnp.arange(tokens_here)[:, None] < jnp.arange(tokens_here)[None, :]
    ).astype(jnp.float32)
    rank = jnp.dot(named, later, preferred_element_type=jnp.float32)
    load = jnp.sum(named, axis=1)
    is_host = jnp.sum((helpers[:, None] == experts[None, :]).astype(jnp.float32), axis=0)
    free = jnp.sum(is_host * (capacity - jnp.minimum(load, capacity)))
    limit = capacity + jnp.where(experts == popular, free, 0.0)
    weight = jnp.sum(jnp.where(hits, gates.T[:, None, :], 0.0), axis=0)
    return jnp.where(rank < limit[:, None], weight, 0.0)


def norm_kernel(*refs):
    values, extras, gain, out = refs[0], refs[1:-2], refs[-2], refs[-1]
    count = values.shape[0]
    floats = values[...].astype(jnp.float32)
    inverse_rms = lax.rsqrt(jnp.mean(floats * floats, axis=-1, keepdims=True) + EPSILON)
    out[pl.ds(0, count), :] = (floats * inverse_rms * gain[...]).astype(out.dtype)
    for index, extra in enumerate(extras):
        out[pl.ds((index + 1) * count, count), :] = extra[...]


def norm_call(arrays, gain_row):
    count, features = arrays[0].shape
    shape = (len(arrays) * count, features)
    return pl.pallas_call(
        norm_kernel,
        out_shape=jax.ShapeDtypeStruct(shape, jnp.bfloat16),
        cost_estimate=pl.CostEstimate(
            flops=4 * count * features,
            bytes_accessed=4 * len(arrays) * count * features,
            transcendentals=0,
        ),
        name="norm",
    )(*arrays, gain_row)


def column_of(table, column):
    lanes = lax.broadcasted_iota(jnp.int32, table.shape, 1)
    return jnp.sum(jnp.where(lanes == column, table, 0.0), axis=1, keepdims=True)


def across(left, right):
    return lax.dot_general(
        left, right, (((1,), (1,)), ((), ())), preferred_element_type=jnp.float32
    )


def run_experts(info, step, tiles, own, mate, one_tile, finish):
    for member, weights in enumerate((own, mate)):

        @pl.when((step >= member * tiles) & (step < (member + 1) * tiles))
        def _():
            one_tile(weights, info[member], step == member * tiles)

    for member in range(2):

        @pl.when(step == member * tiles + tiles - 1)
        def _():
            finish(info[member], member == 0)


def load_parts(info, parts, places, table):
    offset = 0
    for stack, gates in parts:
        count = gates[0].shape[1]
        window = pl.ds(offset, count)
        for index, place in enumerate(places):
            source = pl.ds(index * count, count)
            value = stack[0][source, :]
            if len(stack) == 2:
                value = jnp.where(info[2] > 0, stack[1][source, :], value)
            place[window, :] = value
        value = gates[0][...]
        if len(gates) == 2:
            value = jnp.where(info[2] > 0, gates[1][...], value)
        spare = jnp.zeros((count - value.shape[0], count), value.dtype)
        table[window, :] = jnp.concatenate([value, spare], axis=0).T
        offset += count


def store_parts(value, outs):
    offset = 0
    for out in outs:
        count = out.shape[0]
        out[...] = value[offset : offset + count].astype(out.dtype)
        offset += count


def forward_kernel(tiles, info, parts, gain, own, mate, outs, rows, table, acc, total):
    step = pl.program_id(0)

    @pl.when(step == 0)
    def _():
        load_parts(info, parts, (rows,), table)

    def one_tile(weights, expert, first):
        gate_pre = across(rows[...], weights[0])
        up_pre = across(rows[...], weights[1])
        hidden = (gate_pre * (1.0 / (1.0 + jnp.exp(-gate_pre))) * up_pre).astype(jnp.bfloat16)
        part = jnp.dot(hidden, weights[2], preferred_element_type=jnp.float32)
        acc[...] = jnp.where(first, part, acc[...] + part)

    def finish(expert, first):
        gate = column_of(table[...], expert)
        part = gate * acc[...].astype(jnp.bfloat16).astype(jnp.float32)
        if first:
            total[...] = part
        else:
            store_parts(total[...] + part, outs)

    run_experts(info, step, tiles, own, mate, one_tile, finish)


def backward_kernel(tiles, info, parts, gain, own, mate, outs, rows, grad, table, scaled, acc, total):
    step = pl.program_id(0)
    half = parts[0][-1][0].shape[0] // 2

    @pl.when(step == 0)
    def _():
        load_parts(info, parts, (rows, grad), table)

    def one_tile(weights, expert, first):
        @pl.when(first)
        def _():
            gate = column_of(table[...], half + expert)
            scaled[...] = (gate * grad[...].astype(jnp.float32)).astype(jnp.bfloat16)

        gate_pre = across(rows[...], weights[0])
        up_pre = across(rows[...], weights[1])
        back_hidden = across(scaled[...], weights[2])
        sig = 1.0 / (1.0 + jnp.exp(-gate_pre))
        d_gate = (back_hidden * up_pre * sig * (1.0 + gate_pre * (1.0 - sig))).astype(jnp.bfloat16)
        d_up = (back_hidden * gate_pre * sig).astype(jnp.bfloat16)
        part = jnp.dot(d_gate, weights[0], preferred_element_type=jnp.float32) + jnp.dot(
            d_up, weights[1], preferred_element_type=jnp.float32
        )
        acc[...] = jnp.where(first, part, acc[...] + part)

    def finish(expert, first):
        part = acc[...].astype(jnp.bfloat16).astype(jnp.float32)
        if first:
            total[...] = part
        else:
            store_parts(gain[...] * (total[...] + part), outs)

    run_experts(info, step, tiles, own, mate, one_tile, finish)


def expert_call(info, parts, gain_row, own, mate):
    features = parts[0][0][0].shape[1]
    counts = [gates[0].shape[1] for _, gates in parts]
    backward = parts[0][0][0].shape[0] > counts[0]
    total = sum(counts)
    hidden = own.shape[1]
    width = 256 if hidden % 256 == 0 else hidden
    tiles = hidden // width
    flat = [member for part in parts for pair in part for member in pair]

    def whole(value):
        return pl.BlockSpec(value.shape, lambda s, i: (0, 0))

    own_spec = pl.BlockSpec((3, width, features), lambda s, i: (0, jnp.minimum(s, tiles - 1), 0))
    mate_spec = pl.BlockSpec((3, width, features), lambda s, i: (0, jnp.maximum(s - tiles, 0), 0))
    rows = pltpu.VMEM((total, features), jnp.bfloat16)
    wide = pltpu.VMEM((total, features), jnp.float32)
    table = pltpu.VMEM((total, counts[0]), jnp.float32)
    if backward:
        kernel, scratch, matmuls = backward_kernel, [rows, rows, table, rows, wide, wide], 5
    else:
        kernel, scratch, matmuls = forward_kernel, [rows, table, wide, wide], 3

    def body(info_ref, *refs):
        ins, rest = list(refs[: len(flat)]), refs[len(flat) :]
        nested = [[[ins.pop(0) for _ in pair] for pair in part] for part in parts]
        outs = rest[3 : 3 + len(parts)]
        kernel(tiles, info_ref, nested, *rest[:3], outs, *rest[3 + len(parts) :])

    shapes = [
        jax.ShapeDtypeStruct((count, features), jnp.bfloat16) for count in counts
    ]
    return pl.pallas_call(
        body,
        out_shape=shapes,
        grid_spec=pltpu.PrefetchScalarGridSpec(
            num_scalar_prefetch=1,
            grid=(2 * tiles,),
            in_specs=[whole(value) for value in [*flat, gain_row]] + [own_spec, mate_spec],
            out_specs=[whole(shape) for shape in shapes],
            scratch_shapes=scratch,
        ),
        cost_estimate=pl.CostEstimate(
            flops=2 * matmuls * 2 * total * hidden * features,
            bytes_accessed=2 * 2 * own.size,
            transcendentals=2 * total * hidden,
        ),
        compiler_params=pltpu.CompilerParams(vmem_limit_bytes=50 * 1024 * 1024),
        name="back" if backward else "fore",
    )(info, *flat, gain_row, own, mate)


def add_rows(left, right):
    return (left.astype(jnp.float32) + right.astype(jnp.float32)).astype(jnp.bfloat16)


def after(value, other):
    return lax.optimization_barrier((value, other))[0]


def gather_shards(
    fwd_in,
    route_fwd,
    gate_fwd,
    bwd_in,
    bwd_grad,
    route_bwd,
    gate_bwd,
    replica_plan,
    norm_gain,
    expert_weights,
):
    devices = lax.axis_size("expert")
    position = lax.axis_index("expert")
    tokens_here = fwd_in.shape[1]
    top_count = route_fwd.shape[2]
    capacity = 3 * tokens_here * top_count // (2 * devices)
    popular = replica_plan[0, 0]
    helpers = replica_plan[0, 1:]
    resident = expert_weights[0, 0]
    gain_row = norm_gain
    mate = lax.ppermute(resident, "expert", [(i, i ^ 1) for i in range(devices)])
    table = jnp.concatenate(
        [
            accepted_gates(route_fwd[0], gate_fwd[0], popular, helpers, devices, capacity),
            accepted_gates(route_bwd[0], gate_bwd[0], popular, helpers, devices, capacity),
        ],
        axis=0,
    )
    table_near = along_line(table, NEAR)
    table_two = along_line(table, TWO_AWAY)
    table_mirror = along_line(table, MIRROR)
    at_end = ((position < 2) | (position >= devices - 2)).astype(jnp.int32)
    info = (
        position * jnp.array([1, 1, 0], jnp.int32)
        + (1 - 2 * (position % 2)) * jnp.array([0, 1, 0], jnp.int32)
        + at_end * jnp.array([0, 0, 1], jnp.int32)
    )
    second_table, third_table = (table_mirror, table_two), (table_two, table_mirror)

    grads = bwd_grad[0]
    rows_b = norm_call((bwd_in[0], grads), gain_row)
    rows_f = norm_call((fwd_in[0],), gain_row)
    ahead_in = to_section(fwd_in[0], HERE, 1)
    behind_in = to_section(bwd_in[0], HERE, -1)
    behind_grad = to_section(grads, HERE, -1)

    near_rows = along_line(rows_b, NEAR)
    middle_rows = along_line(rows_b, MIDDLE)
    inner_rows = along_line(near_rows, MIDDLE)
    outer_one_rows = along_line(middle_rows, OUTWARD)
    outer_two_rows = along_line(inner_rows, OUTWARD)
    own_b, near_b = expert_call(
        info, (((rows_b,), (table,)), ((near_rows,), (table_near,))), gain_row, resident, mate
    )
    (second_b,) = expert_call(
        info, (((middle_rows, outer_one_rows), second_table),), gain_row, resident, mate
    )
    (third_b,) = expert_call(
        info, (((inner_rows, outer_two_rows), third_table),), gain_row, resident, mate
    )

    near_f = along_line(rows_f, NEAR)
    middle_f = along_line(rows_f, MIDDLE)
    inner_f = along_line(near_f, MIDDLE)
    outer_one_f = along_line(middle_f, OUTWARD)
    outer_two_f = along_line(inner_f, OUTWARD)
    own_f, back_f, second_f, third_f = expert_call(
        info,
        (
            ((rows_f,), (table,)),
            ((near_f,), (table_near,)),
            ((middle_f, outer_one_f), second_table),
            ((inner_f, outer_two_f), third_table),
        ),
        gain_row,
        resident,
        mate,
    )

    behind_own = to_section(own_b, HERE, -1)
    near_in_b = to_section(near_b, INWARD, -1)
    second_sum_b = add_rows(second_b, along_line(second_b, INWARD))
    second_over_b = to_section(second_sum_b, MIDDLE, -1)
    third_in_b = after(along_line(third_b, INWARD), second_b)
    third_over_b = along_line(add_rows(third_b, third_in_b), MIDDLE)
    near_b = add_rows(near_b, third_over_b)
    near_out_b = to_section(near_b, OUTWARD, -1)
    scaled = (
        (behind_own.astype(jnp.float32) + near_in_b.astype(jnp.float32))
        + near_out_b.astype(jnp.float32)
    ) + second_over_b.astype(jnp.float32)
    prev_grad = (
        behind_grad.astype(jnp.float32) + norm_back(behind_in, 1.0, scaled)
    ).astype(jnp.bfloat16)

    third_in_f = after(along_line(third_f, INWARD), third_b)
    third_over_f = along_line(add_rows(third_f, third_in_f), MIDDLE)
    second_in_f = to_section(second_f, SKIP, 1)
    near_in_f = to_section(back_f, INWARD, 1)
    ahead_own = to_section(own_f, HERE, 1)
    near_out_f = to_section(add_rows(back_f, after(third_over_f, second_b)), OUTWARD, 1)
    second_over_f = to_section(second_f, MIDDLE, 1)
    mixed = (
        (ahead_own.astype(jnp.float32) + near_in_f.astype(jnp.float32))
        + near_out_f.astype(jnp.float32)
    ) + (second_in_f.astype(jnp.float32) + second_over_f.astype(jnp.float32))
    next_in = (ahead_in.astype(jnp.float32) + mixed).astype(jnp.bfloat16)
    return (next_in[None], prev_grad[None])


def exchange_shards(
    fwd_in,
    route_fwd,
    gate_fwd,
    bwd_in,
    bwd_grad,
    route_bwd,
    gate_bwd,
    replica_plan,
    norm_gain,
    expert_weights,
):
    devices = lax.axis_size("expert")
    tokens_here = fwd_in.shape[1]
    features = fwd_in.shape[2]
    top_count = route_fwd.shape[2]
    capacity = 3 * tokens_here * top_count // (2 * devices)
    popular = replica_plan[0, 0]
    helpers = replica_plan[0, 1:]
    resident = expert_weights[0, 0]
    own_weights = (resident[0], resident[1], resident[2])
    gain_row = norm_gain[0]
    normed_fwd = normalize(fwd_in[0], gain_row)
    normed_bwd = normalize(bwd_in[0], gain_row)
    scaled_grad = (gate_bwd[0][:, :, None] * bwd_grad[0].astype(jnp.float32)[:, None, :]).astype(
        jnp.bfloat16
    )
    scaled_grad = scaled_grad.reshape(tokens_here * top_count, features)
    target_fwd, anchor_fwd = place_slots(
        route_fwd[0].reshape(-1), popular, helpers, devices, capacity
    )
    target_bwd, anchor_bwd = place_slots(
        route_bwd[0].reshape(-1), popular, helpers, devices, capacity
    )
    built_fwd, safe_fwd = build_rows(((normed_fwd, top_count),), target_fwd, devices, capacity)
    built_bwd, safe_bwd = build_rows(
        ((normed_bwd, top_count), (scaled_grad, 1)), target_bwd, devices, capacity
    )
    tags_fwd = build_tags(anchor_fwd, safe_fwd, devices, capacity)
    tags_bwd = build_tags(anchor_bwd, safe_bwd, devices, capacity)
    recv_fwd, recv_tags_fwd = (
        lax.all_to_all(built_fwd[0], "expert", split_axis=0, concat_axis=0, tiled=True),
        lax.all_to_all(tags_fwd, "expert", split_axis=0, concat_axis=0, tiled=True),
    )
    recv_bwd, recv_grad, recv_tags_bwd = (
        lax.all_to_all(built_bwd[0], "expert", split_axis=0, concat_axis=0, tiled=True),
        lax.all_to_all(built_bwd[1], "expert", split_axis=0, concat_axis=0, tiled=True),
        lax.all_to_all(tags_bwd, "expert", split_axis=0, concat_axis=0, tiled=True),
    )
    fetched = broadcast(resident, "expert", popular)
    hot_weights = (fetched[0], fetched[1], fetched[2])
    slot_total = devices * capacity
    out_fwd = grouped(
        expert_forward,
        (recv_fwd.reshape(slot_total, features),),
        recv_tags_fwd.reshape(slot_total),
        own_weights,
        hot_weights,
    )
    back_fwd = lax.all_to_all(
        out_fwd.reshape(devices, capacity, features),
        "expert",
        split_axis=0,
        concat_axis=0,
        tiled=True,
    )
    expert_out = collect(back_fwd, target_fwd, tokens_here, top_count)
    mixed = jnp.sum(gate_fwd[0][:, :, None] * expert_out.astype(jnp.float32), axis=1)
    layer_out = (fwd_in[0].astype(jnp.float32) + mixed).astype(jnp.bfloat16)
    next_in = from_behind(layer_out, "pipe", 1)
    out_bwd = grouped(
        expert_backward,
        (recv_bwd.reshape(slot_total, features), recv_grad.reshape(slot_total, features)),
        recv_tags_bwd.reshape(slot_total),
        own_weights,
        hot_weights,
    )
    back_bwd = lax.all_to_all(
        out_bwd.reshape(devices, capacity, features),
        "expert",
        split_axis=0,
        concat_axis=0,
        tiled=True,
    )
    slot_grad = collect(back_bwd, target_bwd, tokens_here, top_count)
    normed_grad = jnp.sum(slot_grad.astype(jnp.float32), axis=1)
    input_grad = (
        bwd_grad[0].astype(jnp.float32) + norm_back(bwd_in[0], gain_row, normed_grad)
    ).astype(jnp.bfloat16)
    prev_grad = from_behind(input_grad, "pipe", -1)
    return (next_in[None], prev_grad[None])


def solution(mesh):
    in_specs = (
        P("pipe", "expert", None),
        P("pipe", "expert", None),
        P("pipe", "expert", None),
        P("pipe", "expert", None),
        P("pipe", "expert", None),
        P("pipe", "expert", None),
        P("pipe", "expert", None),
        P("pipe", None),
        P("pipe", None),
        P("pipe", "expert", None, None, None),
    )
    out_specs = (P("pipe", "expert", None), P("pipe", "expert", None))
    gathers = mesh.shape["expert"] == 2 * CHIPS
    plan = gather_shards if gathers else exchange_shards

    return jax.shard_map(plan, mesh=mesh, in_specs=in_specs, out_specs=out_specs, check_vma=False)
```

```python
import jax
import jax.numpy as jnp
from jax import lax
from jax.experimental import pallas as pl
from jax.experimental.pallas import tpu as pltpu
from jax.sharding import PartitionSpec as P

EPSILON = 1e-06


def broadcast(block, axis, owner):
    block = jnp.where(lax.axis_index(axis) == owner, block, jnp.zeros_like(block))
    return lax.psum(block, axis)


def from_behind(value, axis, steps):
    count = lax.axis_size(axis)
    pairs = [(source, (source + steps) % count) for source in range(count)]
    return lax.ppermute(value, axis, pairs)


def normalize(values, norm_scale):
    floats = values.astype(jnp.float32)
    inverse_rms = lax.rsqrt(jnp.mean(floats * floats, axis=-1, keepdims=True) + EPSILON)
    return (floats * inverse_rms * norm_scale).astype(jnp.bfloat16)


def norm_back(values, norm_scale, gradient):
    floats = values.astype(jnp.float32)
    inverse_rms = lax.rsqrt(jnp.mean(floats * floats, axis=-1, keepdims=True) + EPSILON)
    scaled = gradient * norm_scale
    return inverse_rms * scaled - floats * inverse_rms**3 * jnp.mean(
        floats * scaled, axis=-1, keepdims=True
    )


def place_slots(routing, popular, helpers, devices, capacity):
    experts = jnp.arange(devices, dtype=jnp.int32)
    onehot = (routing[:, None] == experts[None, :]).astype(jnp.int32)
    before = jnp.cumsum(onehot, axis=0, dtype=jnp.int32) - onehot
    ranking = jnp.sum(before * onehot, axis=1, dtype=jnp.int32)
    per_expert = jnp.sum(onehot, axis=0, dtype=jnp.int32)
    host_hit = (helpers[:, None] == experts[None, :]).astype(jnp.int32)
    occupied = jnp.minimum(
        jnp.sum(host_hit * per_expert[None, :], axis=1, dtype=jnp.int32), capacity
    )
    spare_rows = capacity - occupied
    spare_ends = jnp.cumsum(spare_rows, dtype=jnp.int32)
    spare_starts = spare_ends - spare_rows
    overflow = ranking - capacity
    host_slot = jnp.sum(
        (overflow[:, None] >= spare_ends[None, :]).astype(jnp.int32), axis=1, dtype=jnp.int32
    )
    home_ok = ranking < capacity
    spill_ok = (routing == popular) & jnp.logical_not(home_ok) & (host_slot < helpers.shape[0])
    chosen = (host_slot[:, None] == jnp.arange(helpers.shape[0], dtype=jnp.int32)[None, :]).astype(
        jnp.int32
    )
    spill_device = jnp.sum(chosen * helpers[None, :], axis=1, dtype=jnp.int32)
    spill_place = (
        jnp.sum(chosen * (occupied - spare_starts)[None, :], axis=1, dtype=jnp.int32) + overflow
    )
    target = jnp.where(home_ok, routing * capacity + ranking, spill_device * capacity + spill_place)
    target = jnp.where(home_ok | spill_ok, target, -1)
    anchor = jnp.where(home_ok, 1, 2).astype(jnp.int32)
    return (target, anchor)


def expert_forward(pieces, weights):
    inputs = pieces[0]
    gate_pre = jnp.einsum("bd,fd->bf", inputs, weights[0], preferred_element_type=jnp.float32)
    up_pre = jnp.einsum("bd,fd->bf", inputs, weights[1], preferred_element_type=jnp.float32)
    sigmoid_gate = 1.0 / (1.0 + jnp.exp(-gate_pre))
    hidden = (gate_pre * sigmoid_gate * up_pre).astype(jnp.bfloat16)
    return jnp.dot(hidden, weights[2], preferred_element_type=jnp.float32).astype(jnp.bfloat16)


def expert_backward(pieces, weights):
    inputs, grad_rows = pieces
    gate_pre = jnp.einsum("bd,fd->bf", inputs, weights[0], preferred_element_type=jnp.float32)
    up_pre = jnp.einsum("bd,fd->bf", inputs, weights[1], preferred_element_type=jnp.float32)
    back_hidden = jnp.einsum("bd,fd->bf", grad_rows, weights[2], preferred_element_type=jnp.float32)
    sigmoid_gate = 1.0 / (1.0 + jnp.exp(-gate_pre))
    d_gate = (back_hidden * up_pre * sigmoid_gate * (1.0 + gate_pre * (1.0 - sigmoid_gate))).astype(
        jnp.bfloat16
    )
    d_up = (back_hidden * gate_pre * sigmoid_gate).astype(jnp.bfloat16)
    summed = jnp.dot(d_gate, weights[0], preferred_element_type=jnp.float32) + jnp.dot(
        d_up, weights[1], preferred_element_type=jnp.float32
    )
    return summed.astype(jnp.bfloat16)


def build_rows(tables, target, devices, capacity):
    count = target.shape[0]
    total = devices * capacity
    safe_target = jnp.where(target >= 0, target, total)
    source_of = (
        jnp.full((total,), -1, jnp.int32)
        .at[safe_target]
        .set(jnp.arange(count, dtype=jnp.int32), mode="drop")
    )
    present = source_of >= 0
    clipped = jnp.maximum(source_of, 0)
    built = []
    for table, stride in tables:
        rows_here = jnp.where(
            present[:, None], table[clipped // stride], jnp.zeros((), table.dtype)
        )
        built.append(rows_here.reshape(devices, capacity, table.shape[-1]))
    return (tuple(built), safe_target)


def build_tags(anchor, safe_target, devices, capacity):
    tags = jnp.zeros((devices * capacity,), jnp.int32).at[safe_target].set(anchor, mode="drop")
    return tags.astype(jnp.bfloat16).reshape(devices, capacity)


def grouped(function, inputs, tags, own_weights, hot_weights):
    total = tags.shape[0]
    features = inputs[0].shape[-1]
    anchor = tags.astype(jnp.int32)
    is_own = anchor == 1
    is_hot = anchor == 2
    is_empty = jnp.logical_not(is_own | is_hot)
    own_count = jnp.sum(is_own.astype(jnp.int32), dtype=jnp.int32)
    hot_count = jnp.sum(is_hot.astype(jnp.int32), dtype=jnp.int32)
    own_rank = jnp.cumsum(is_own.astype(jnp.int32), dtype=jnp.int32) - 1
    hot_rank = own_count + jnp.cumsum(is_hot.astype(jnp.int32), dtype=jnp.int32) - 1
    empty_rank = own_count + hot_count + jnp.cumsum(is_empty.astype(jnp.int32), dtype=jnp.int32) - 1
    position = jnp.where(is_own, own_rank, jnp.where(is_hot, hot_rank, empty_rank))
    ordering = jnp.zeros((total,), jnp.int32).at[position].set(jnp.arange(total, dtype=jnp.int32))
    block = 128
    number = total // block
    stacked = tuple(
        (member[ordering].reshape(number, block, member.shape[-1]) for member in inputs)
    )
    empty_out = jnp.zeros((block, features), jnp.bfloat16)

    def one_block(packed):
        pieces, start = packed
        own_out = lax.cond(
            start < own_count, lambda: function(pieces, own_weights), lambda: empty_out
        )
        needs_hot = (start + block > own_count) & (start < own_count + hot_count)
        hot_out = lax.cond(needs_hot, lambda: function(pieces, hot_weights), lambda: empty_out)
        row_ids = start + jnp.arange(block, dtype=jnp.int32)
        return jnp.where((row_ids < own_count)[:, None], own_out, hot_out)

    starts = jnp.arange(number, dtype=jnp.int32) * block
    outputs = lax.map(one_block, (stacked, starts))
    return outputs.reshape(total, features)[position]


def collect(returned, target, tokens_here, top_count):
    flat_back = returned.reshape(-1, returned.shape[-1])
    limit = flat_back.shape[0]
    picked = flat_back[jnp.clip(target, 0, limit - 1)]
    picked = jnp.where((target >= 0)[:, None], picked, jnp.zeros((), flat_back.dtype))
    return picked.reshape(tokens_here, top_count, flat_back.shape[-1])


CHIPS = 4


def along_line(value, chip_pairs):
    pairs = [(2 * a + core, 2 * b + core) for a, b in chip_pairs for core in range(2)]
    return lax.ppermute(value, "expert", pairs)


def to_section(value, chip_pairs, ahead):
    sections, devices = lax.axis_size("pipe"), lax.axis_size("expert")
    pairs = [
        (section * devices + 2 * a + core, (section + ahead) % sections * devices + 2 * b + core)
        for section in range(sections)
        for a, b in chip_pairs
        for core in range(2)
    ]
    return lax.ppermute(value, ("pipe", "expert"), pairs)


NEAR = ((0, 1), (1, 0), (2, 3), (3, 2))
MIDDLE = ((1, 2), (2, 1))
OUTWARD = ((1, 0), (2, 3))
INWARD = ((0, 1), (3, 2))
HERE = ((0, 0), (1, 1), (2, 2), (3, 3))
SKIP = ((0, 2), (3, 1))
TWO_AWAY = ((0, 2), (2, 0), (1, 3), (3, 1))
MIRROR = ((0, 3), (3, 0), (1, 2), (2, 1))


def accepted_gates(routing, gates, popular, helpers, devices, capacity):
    tokens_here = routing.shape[0]
    experts = jnp.arange(devices, dtype=jnp.int32)
    hits = routing.T[:, None, :] == experts[None, :, None]
    named = jnp.sum(hits.astype(jnp.float32), axis=0)
    later = (
        jnp.arange(tokens_here)[:, None] < jnp.arange(tokens_here)[None, :]
    ).astype(jnp.float32)
    rank = jnp.dot(named, later, preferred_element_type=jnp.float32)
    load = jnp.sum(named, axis=1)
    is_host = jnp.sum((helpers[:, None] == experts[None, :]).astype(jnp.float32), axis=0)
    free = jnp.sum(is_host * (capacity - jnp.minimum(load, capacity)))
    limit = capacity + jnp.where(experts == popular, free, 0.0)
    weight = jnp.sum(jnp.where(hits, gates.T[:, None, :], 0.0), axis=0)
    return jnp.where(rank < limit[:, None], weight, 0.0)


def norm_kernel(*refs):
    values, extras, gain, out = refs[0], refs[1:-2], refs[-2], refs[-1]
    count = values.shape[0]
    floats = values[...].astype(jnp.float32)
    inverse_rms = lax.rsqrt(jnp.mean(floats * floats, axis=-1, keepdims=True) + EPSILON)
    out[pl.ds(0, count), :] = (floats * inverse_rms * gain[...]).astype(out.dtype)
    for index, extra in enumerate(extras):
        out[pl.ds((index + 1) * count, count), :] = extra[...]


def norm_call(arrays, gain_row):
    count, features = arrays[0].shape
    shape = (len(arrays) * count, features)
    return pl.pallas_call(
        norm_kernel,
        out_shape=jax.ShapeDtypeStruct(shape, jnp.bfloat16),
        cost_estimate=pl.CostEstimate(
            flops=4 * count * features,
            bytes_accessed=4 * len(arrays) * count * features,
            transcendentals=0,
        ),
        name="norm",
    )(*arrays, gain_row)


def finish_kernel(rows, grad, *refs):
    sums, out = refs[:-1], refs[-1]
    scaled = sums[0][...].astype(jnp.float32)
    for part in sums[1:]:
        scaled += part[...].astype(jnp.float32)
    back = norm_back(rows[...], 1.0, scaled)
    out[...] = (grad[...].astype(jnp.float32) + back).astype(out.dtype)


def finish_call(rows, grad, sums):
    return pl.pallas_call(
        finish_kernel,
        out_shape=jax.ShapeDtypeStruct(rows.shape, jnp.bfloat16),
        cost_estimate=pl.CostEstimate(
            flops=12 * rows.size, bytes_accessed=14 * rows.size, transcendentals=0
        ),
        name="finish",
    )(rows, grad, *sums)


def column_of(table, column):
    lanes = lax.broadcasted_iota(jnp.int32, table.shape, 1)
    return jnp.sum(jnp.where(lanes == column, table, 0.0), axis=1, keepdims=True)


def across(left, right):
    return lax.dot_general(
        left, right, (((1,), (1,)), ((), ())), preferred_element_type=jnp.float32
    )


def run_experts(info, step, tiles, own, mate, one_tile, finish):
    for member, weights in enumerate((own, mate)):

        @pl.when((step >= member * tiles) & (step < (member + 1) * tiles))
        def _():
            one_tile(weights, info[member], step == member * tiles)

    for member in range(2):

        @pl.when(step == member * tiles + tiles - 1)
        def _():
            finish(info[member], member == 0)


def load_parts(info, parts, places, table):
    offset = 0
    for stack, gates in parts:
        count = gates[0].shape[1]
        window = pl.ds(offset, count)
        for index, place in enumerate(places):
            source = pl.ds(index * count, count)
            value = stack[0][source, :]
            if len(stack) == 2:
                value = jnp.where(info[2] > 0, stack[1][source, :], value)
            place[window, :] = value
        value = gates[0][...]
        if len(gates) == 2:
            value = jnp.where(info[2] > 0, gates[1][...], value)
        spare = jnp.zeros((count - value.shape[0], count), value.dtype)
        table[window, :] = jnp.concatenate([value, spare], axis=0).T
        offset += count


def store_parts(value, outs):
    offset = 0
    for out in outs:
        count = out.shape[0]
        out[...] = value[offset : offset + count].astype(out.dtype)
        offset += count


def forward_kernel(tiles, info, parts, gain, own, mate, outs, rows, table, acc, total):
    step = pl.program_id(0)

    @pl.when(step == 0)
    def _():
        load_parts(info, parts, (rows,), table)

    def one_tile(weights, expert, first):
        gate_pre = across(rows[...], weights[0])
        up_pre = across(rows[...], weights[1])
        hidden = (gate_pre * (1.0 / (1.0 + jnp.exp(-gate_pre))) * up_pre).astype(jnp.bfloat16)
        part = jnp.dot(hidden, weights[2], preferred_element_type=jnp.float32)
        acc[...] = jnp.where(first, part, acc[...] + part)

    def finish(expert, first):
        gate = column_of(table[...], expert)
        part = gate * acc[...].astype(jnp.bfloat16).astype(jnp.float32)
        if first:
            total[...] = part
        else:
            store_parts(total[...] + part, outs)

    run_experts(info, step, tiles, own, mate, one_tile, finish)


def backward_kernel(tiles, info, parts, gain, own, mate, outs, rows, grad, table, scaled, acc, total):
    step = pl.program_id(0)
    half = parts[0][-1][0].shape[0] // 2

    @pl.when(step == 0)
    def _():
        load_parts(info, parts, (rows, grad), table)

    def one_tile(weights, expert, first):
        @pl.when(first)
        def _():
            gate = column_of(table[...], half + expert)
            scaled[...] = (gate * grad[...].astype(jnp.float32)).astype(jnp.bfloat16)

        gate_pre = across(rows[...], weights[0])
        up_pre = across(rows[...], weights[1])
        back_hidden = across(scaled[...], weights[2])
        sig = 1.0 / (1.0 + jnp.exp(-gate_pre))
        d_gate = (back_hidden * up_pre * sig * (1.0 + gate_pre * (1.0 - sig))).astype(jnp.bfloat16)
        d_up = (back_hidden * gate_pre * sig).astype(jnp.bfloat16)
        part = jnp.dot(d_gate, weights[0], preferred_element_type=jnp.float32) + jnp.dot(
            d_up, weights[1], preferred_element_type=jnp.float32
        )
        acc[...] = jnp.where(first, part, acc[...] + part)

    def finish(expert, first):
        part = acc[...].astype(jnp.bfloat16).astype(jnp.float32)
        if first:
            total[...] = part
        else:
            store_parts(gain[...] * (total[...] + part), outs)

    run_experts(info, step, tiles, own, mate, one_tile, finish)


def expert_call(info, parts, gain_row, own, mate):
    features = parts[0][0][0].shape[1]
    counts = [gates[0].shape[1] for _, gates in parts]
    backward = parts[0][0][0].shape[0] > counts[0]
    total = sum(counts)
    hidden = own.shape[1]
    width = 256 if hidden % 256 == 0 else hidden
    tiles = hidden // width
    flat = [member for part in parts for pair in part for member in pair]

    def whole(value):
        return pl.BlockSpec(value.shape, lambda s, i: (0, 0))

    own_spec = pl.BlockSpec((3, width, features), lambda s, i: (0, jnp.minimum(s, tiles - 1), 0))
    mate_spec = pl.BlockSpec((3, width, features), lambda s, i: (0, jnp.maximum(s - tiles, 0), 0))
    rows = pltpu.VMEM((total, features), jnp.bfloat16)
    wide = pltpu.VMEM((total, features), jnp.float32)
    table = pltpu.VMEM((total, counts[0]), jnp.float32)
    if backward:
        kernel, scratch, matmuls = backward_kernel, [rows, rows, table, rows, wide, wide], 5
    else:
        kernel, scratch, matmuls = forward_kernel, [rows, table, wide, wide], 3

    def body(info_ref, *refs):
        ins, rest = list(refs[: len(flat)]), refs[len(flat) :]
        nested = [[[ins.pop(0) for _ in pair] for pair in part] for part in parts]
        outs = rest[3 : 3 + len(parts)]
        kernel(tiles, info_ref, nested, *rest[:3], outs, *rest[3 + len(parts) :])

    shapes = [
        jax.ShapeDtypeStruct((count, features), jnp.bfloat16) for count in counts
    ]
    return pl.pallas_call(
        body,
        out_shape=shapes,
        grid_spec=pltpu.PrefetchScalarGridSpec(
            num_scalar_prefetch=1,
            grid=(2 * tiles,),
            in_specs=[whole(value) for value in [*flat, gain_row]] + [own_spec, mate_spec],
            out_specs=[whole(shape) for shape in shapes],
            scratch_shapes=scratch,
        ),
        cost_estimate=pl.CostEstimate(
            flops=2 * matmuls * 2 * total * hidden * features,
            bytes_accessed=2 * 2 * own.size,
            transcendentals=2 * total * hidden,
        ),
        compiler_params=pltpu.CompilerParams(vmem_limit_bytes=50 * 1024 * 1024),
        name="back" if backward else "fore",
    )(info, *flat, gain_row, own, mate)


def add_rows(left, right):
    return (left.astype(jnp.float32) + right.astype(jnp.float32)).astype(jnp.bfloat16)


def after(value, other):
    return lax.optimization_barrier((value, other))[0]


def gather_shards(
    fwd_in,
    route_fwd,
    gate_fwd,
    bwd_in,
    bwd_grad,
    route_bwd,
    gate_bwd,
    replica_plan,
    norm_gain,
    expert_weights,
):
    devices = lax.axis_size("expert")
    position = lax.axis_index("expert")
    tokens_here = fwd_in.shape[1]
    top_count = route_fwd.shape[2]
    capacity = 3 * tokens_here * top_count // (2 * devices)
    popular = replica_plan[0, 0]
    helpers = replica_plan[0, 1:]
    resident = expert_weights[0, 0]
    gain_row = norm_gain
    mate = lax.ppermute(resident, "expert", [(i, i ^ 1) for i in range(devices)])
    table = jnp.concatenate(
        [
            accepted_gates(route_fwd[0], gate_fwd[0], popular, helpers, devices, capacity),
            accepted_gates(route_bwd[0], gate_bwd[0], popular, helpers, devices, capacity),
        ],
        axis=0,
    )
    table_near = along_line(table, NEAR)
    table_two = along_line(table, TWO_AWAY)
    table_mirror = along_line(table, MIRROR)
    at_end = ((position < 2) | (position >= devices - 2)).astype(jnp.int32)
    info = (
        position * jnp.array([1, 1, 0], jnp.int32)
        + (1 - 2 * (position % 2)) * jnp.array([0, 1, 0], jnp.int32)
        + at_end * jnp.array([0, 0, 1], jnp.int32)
    )
    second_table, third_table = (table_mirror, table_two), (table_two, table_mirror)

    grads = bwd_grad[0]
    rows_b = norm_call((bwd_in[0], grads), gain_row)
    rows_f = norm_call((fwd_in[0],), gain_row)
    ahead_in = to_section(fwd_in[0], HERE, 1)
    behind_in = to_section(bwd_in[0], HERE, -1)
    behind_grad = to_section(grads, HERE, -1)

    near_rows = along_line(rows_b, NEAR)
    middle_rows = along_line(rows_b, MIDDLE)
    inner_rows = along_line(near_rows, MIDDLE)
    outer_one_rows = along_line(middle_rows, OUTWARD)
    outer_two_rows = along_line(inner_rows, OUTWARD)
    (own_b,) = expert_call(info, (((rows_b,), (table,)),), gain_row, resident, mate)
    (near_b,) = expert_call(info, (((near_rows,), (table_near,)),), gain_row, resident, mate)
    (second_b,) = expert_call(
        info, (((middle_rows, outer_one_rows), second_table),), gain_row, resident, mate
    )
    (third_b,) = expert_call(
        info, (((inner_rows, outer_two_rows), third_table),), gain_row, resident, mate
    )

    near_f = along_line(rows_f, NEAR)
    middle_f = along_line(rows_f, MIDDLE)
    inner_f = along_line(near_f, MIDDLE)
    outer_one_f = along_line(middle_f, OUTWARD)
    outer_two_f = along_line(inner_f, OUTWARD)
    own_f, back_f, second_f, third_f = expert_call(
        info,
        (
            ((rows_f,), (table,)),
            ((near_f,), (table_near,)),
            ((middle_f, outer_one_f), second_table),
            ((inner_f, outer_two_f), third_table),
        ),
        gain_row,
        resident,
        mate,
    )

    behind_own = to_section(own_b, HERE, -1)
    near_in_b = to_section(near_b, INWARD, -1)
    second_sum_b = add_rows(second_b, along_line(second_b, INWARD))
    second_over_b = to_section(second_sum_b, MIDDLE, -1)
    third_in_b = after(along_line(third_b, INWARD), second_b)
    third_over_b = along_line(add_rows(third_b, third_in_b), MIDDLE)
    near_b = add_rows(near_b, third_over_b)
    near_out_b = to_section(near_b, OUTWARD, -1)
    prev_grad = finish_call(
        behind_in, behind_grad, (behind_own, near_in_b, second_over_b, near_out_b)
    )

    third_in_f = after(along_line(third_f, INWARD), third_b)
    third_over_f = along_line(add_rows(third_f, third_in_f), MIDDLE)
    second_in_f = to_section(second_f, SKIP, 1)
    near_in_f = to_section(back_f, INWARD, 1)
    ahead_own = to_section(own_f, HERE, 1)
    near_out_f = to_section(add_rows(back_f, after(third_over_f, second_b)), OUTWARD, 1)
    second_over_f = to_section(second_f, MIDDLE, 1)
    mixed = (
        (ahead_own.astype(jnp.float32) + near_in_f.astype(jnp.float32))
        + near_out_f.astype(jnp.float32)
    ) + (second_in_f.astype(jnp.float32) + second_over_f.astype(jnp.float32))
    next_in = (ahead_in.astype(jnp.float32) + mixed).astype(jnp.bfloat16)
    return (next_in[None], prev_grad[None])


def exchange_shards(
    fwd_in,
    route_fwd,
    gate_fwd,
    bwd_in,
    bwd_grad,
    route_bwd,
    gate_bwd,
    replica_plan,
    norm_gain,
    expert_weights,
):
    devices = lax.axis_size("expert")
    tokens_here = fwd_in.shape[1]
    features = fwd_in.shape[2]
    top_count = route_fwd.shape[2]
    capacity = 3 * tokens_here * top_count // (2 * devices)
    popular = replica_plan[0, 0]
    helpers = replica_plan[0, 1:]
    resident = expert_weights[0, 0]
    own_weights = (resident[0], resident[1], resident[2])
    gain_row = norm_gain[0]
    normed_fwd = normalize(fwd_in[0], gain_row)
    normed_bwd = normalize(bwd_in[0], gain_row)
    scaled_grad = (gate_bwd[0][:, :, None] * bwd_grad[0].astype(jnp.float32)[:, None, :]).astype(
        jnp.bfloat16
    )
    scaled_grad = scaled_grad.reshape(tokens_here * top_count, features)
    target_fwd, anchor_fwd = place_slots(
        route_fwd[0].reshape(-1), popular, helpers, devices, capacity
    )
    target_bwd, anchor_bwd = place_slots(
        route_bwd[0].reshape(-1), popular, helpers, devices, capacity
    )
    built_fwd, safe_fwd = build_rows(((normed_fwd, top_count),), target_fwd, devices, capacity)
    built_bwd, safe_bwd = build_rows(
        ((normed_bwd, top_count), (scaled_grad, 1)), target_bwd, devices, capacity
    )
    tags_fwd = build_tags(anchor_fwd, safe_fwd, devices, capacity)
    tags_bwd = build_tags(anchor_bwd, safe_bwd, devices, capacity)
    recv_fwd, recv_tags_fwd = (
        lax.all_to_all(built_fwd[0], "expert", split_axis=0, concat_axis=0, tiled=True),
        lax.all_to_all(tags_fwd, "expert", split_axis=0, concat_axis=0, tiled=True),
    )
    recv_bwd, recv_grad, recv_tags_bwd = (
        lax.all_to_all(built_bwd[0], "expert", split_axis=0, concat_axis=0, tiled=True),
        lax.all_to_all(built_bwd[1], "expert", split_axis=0, concat_axis=0, tiled=True),
        lax.all_to_all(tags_bwd, "expert", split_axis=0, concat_axis=0, tiled=True),
    )
    fetched = broadcast(resident, "expert", popular)
    hot_weights = (fetched[0], fetched[1], fetched[2])
    slot_total = devices * capacity
    out_fwd = grouped(
        expert_forward,
        (recv_fwd.reshape(slot_total, features),),
        recv_tags_fwd.reshape(slot_total),
        own_weights,
        hot_weights,
    )
    back_fwd = lax.all_to_all(
        out_fwd.reshape(devices, capacity, features),
        "expert",
        split_axis=0,
        concat_axis=0,
        tiled=True,
    )
    expert_out = collect(back_fwd, target_fwd, tokens_here, top_count)
    mixed = jnp.sum(gate_fwd[0][:, :, None] * expert_out.astype(jnp.float32), axis=1)
    layer_out = (fwd_in[0].astype(jnp.float32) + mixed).astype(jnp.bfloat16)
    next_in = from_behind(layer_out, "pipe", 1)
    out_bwd = grouped(
        expert_backward,
        (recv_bwd.reshape(slot_total, features), recv_grad.reshape(slot_total, features)),
        recv_tags_bwd.reshape(slot_total),
        own_weights,
        hot_weights,
    )
    back_bwd = lax.all_to_all(
        out_bwd.reshape(devices, capacity, features),
        "expert",
        split_axis=0,
        concat_axis=0,
        tiled=True,
    )
    slot_grad = collect(back_bwd, target_bwd, tokens_here, top_count)
    normed_grad = jnp.sum(slot_grad.astype(jnp.float32), axis=1)
    input_grad = (
        bwd_grad[0].astype(jnp.float32) + norm_back(bwd_in[0], gain_row, normed_grad)
    ).astype(jnp.bfloat16)
    prev_grad = from_behind(input_grad, "pipe", -1)
    return (next_in[None], prev_grad[None])


def solution(mesh):
    in_specs = (
        P("pipe", "expert", None),
        P("pipe", "expert", None),
        P("pipe", "expert", None),
        P("pipe", "expert", None),
        P("pipe", "expert", None),
        P("pipe", "expert", None),
        P("pipe", "expert", None),
        P("pipe", None),
        P("pipe", None),
        P("pipe", "expert", None, None, None),
    )
    out_specs = (P("pipe", "expert", None), P("pipe", "expert", None))
    gathers = mesh.shape["expert"] == 2 * CHIPS
    plan = gather_shards if gathers else exchange_shards

    return jax.shard_map(plan, mesh=mesh, in_specs=in_specs, out_specs=out_specs, check_vma=False)
```
